32 devices in a mesh: dp: 4 (over z), ctx: 2 (over y), tensor: 4 (over x, core).
Axes of the slice: x: 2, y: 2, z: 4, core: 2. Of those that a mesh axis runs over, the one named last changes fastest.
Arguments:
- tokens: bfloat16 [4096, 2048], P(('dp', 'ctx')), may hold values from -6 to 6
- segments: int32 [4, 1024], P('dp'), may hold values from 0 to 7, never falling along the last dimension, each value on 1 to 512 neighbouring positions
- routes: int32 [4096, 8], P(('dp', 'ctx')), may hold values from 0 to 15, all different within a row; in each aligned block of 512 rows (0 to 511, 512 to 1023, ...) at most 384 rows name the same one
- cotangent: bfloat16 [4096, 2048], P(('dp', 'ctx')), may hold values from -6 to 6
- norm_gain: float32 [2048], replicated, may hold values from 0.5 to 1.5
- post_gain: float32 [2048], replicated, may hold values from 0.5 to 1.5
- query_gain: float32 [128], replicated, may hold values from 0.5 to 1.5
- key_gain: float32 [128], replicated, may hold values from 0.5 to 1.5
- w_query: bfloat16 [2048, 2048], P('dp', 'tensor'), may hold values from -0.125 to 0.125
- w_key: bfloat16 [2048, 2048], P('dp', 'tensor'), may hold values from -0.125 to 0.125
- w_value: bfloat16 [2048, 2048], P('dp', 'tensor'), may hold values from -0.125 to 0.125
- w_output: bfloat16 [2048, 2048], P('dp', 'tensor'), may hold values from -1.5 to 1.5
- w_router: bfloat16 [2048, 16], replicated, may hold values from -0.0625 to 0.0625
- w_gate: bfloat16 [2048, 16, 1024], P('dp', None, 'tensor'), may hold values from -0.125 to 0.125
- w_up: bfloat16 [2048, 16, 1024], P('dp', None, 'tensor'), may hold values from -0.125 to 0.125
- w_down: bfloat16 [2048, 16, 1024], P('dp', None, 'tensor'), may hold values from -1.5 to 1.5
Outputs:
- output: float32 [4096, 2048], P(('dp', 'ctx'))
- input_grad: float32 [4096, 2048], P(('dp', 'ctx'))
- grad_norm_gain: float32 [2048], replicated
- grad_post_gain: float32 [2048], replicated
- grad_query_gain: float32 [128], replicated
- grad_key_gain: float32 [128], replicated
- grad_query: float32 [2048, 2048], P(('dp', 'ctx'), 'tensor')
- grad_key: float32 [2048, 2048], P(('dp', 'ctx'), 'tensor')
- grad_value: float32 [2048, 2048], P(('dp', 'ctx'), 'tensor')
- grad_output: float32 [2048, 2048], P(('dp', 'ctx'), 'tensor')
- grad_router: float32 [2048, 16], replicated
- grad_gate: float32 [2048, 16, 1024], P(('dp', 'ctx'), None, 'tensor')
- grad_up: float32 [2048, 16, 1024], P(('dp', 'ctx'), None, 'tensor')
- grad_down: float32 [2048, 16, 1024], P(('dp', 'ctx'), None, 'tensor')
The draws below stay inside these ranges and needn't reach their ends.
Inputs may be any that keep to these rules, and one draw needn't show every extreme that they name: `routes`: in each aligned block of 512 rows (the rows of one device) no expert is named by more than 384 rows, a bound that some block reaches; the 8 numbers of a row differ. `segments`: in each sequence the document numbers never fall; a document has 1 to 512 positions, and one has exactly 512.
All inputs are finite; a program needn't handle non-finite values.
Results may differ from the reference program's by a relative error of at most 0.024.
Values may be sent and summed in bfloat16 or wider, within the bound.
No kernel may reach another device: no remote copies, remote signals or barrier semaphores. Data moves between devices by JAX's collectives and lax.ppermute only.
A program may use at most 384 MiB of HBM per device.

```python
import math
import jax
import jax.numpy as jnp
import numpy as np
from jax import lax

D = 2048
H = 16
HD = 128
FFE = 1024
TOP = 8
E = 16
DOCS = 8
LEN = 1024
ROWS = 512
TOKENS = 4096
CAP = 384
N_DP = 4


def strengthened(array, rng, source, target, shards_of, factor):
    owner, partner = [(jnp.arange(array.shape[dim]) // (array.shape[dim] // shards_of)).reshape([-1 if axis == dim else 1 for axis in range(array.ndim)]) for dim in (source, target)]
    chosen = jax.random.permutation(rng, shards_of)[partner]
    strong = (owner == chosen) | (owner == (partner + shards_of // 2) % shards_of)
    return jnp.where(strong, factor * array, array)


def steps_of(key, dims, cuts, smallest, largest):
    gain = 1.0
    for dim, blocks in cuts:
        draws = jax.random.uniform(jax.random.fold_in(jax.random.fold_in(key, 6), dim), (blocks,), jnp.float32, smallest / len(cuts), largest / len(cuts))
        gain = gain * jnp.repeat(jnp.exp(draws), dims[dim] // blocks).reshape((-1,) + (1,) * (len(dims) - 1 - dim))
    return gain


def split_up(count, total, most, lean):
    loads = [(1 << 20) // math.isqrt(standing ** lean) + 1 for standing in range(2, count + 1)]
    rest, counts = total - most - (count - 1), [1] * (count - 1)
    while rest > 0:
        free = [i for i in range(count - 1) if counts[i] < most]
        whole, left = sum([loads[i] for i in free]), rest
        for i in free:
            more = min(most - counts[i], max(1, left * loads[i] // whole), rest)
            counts[i] = counts[i] + more
            rest = rest - more
    return np.array([most] + counts)


def ragged(key, count, total, reach, skew):
    if count == 2:
        one = jax.random.randint(key, (), max(1, total - reach), min(reach, total - 1) + 1)
        return jnp.stack([one, total - one])
    lengths = jnp.asarray(split_up(count, total, reach, skew), jnp.int32)
    pairs = (count - 1) // 2
    giver, sink = lengths[1:1 + 2 * pairs:2], lengths[2:2 + 2 * pairs:2]
    room = jnp.minimum(giver - 1, reach - sink)
    shifted = jax.random.randint(jax.random.fold_in(key, 1), (pairs,), 0, 1 << 20) % (room + 1)
    lengths = lengths.at[1:1 + 2 * pairs:2].set(giver - shifted).at[2:2 + 2 * pairs:2].set(sink + shifted)
    return lengths[jax.random.permutation(jax.random.fold_in(key, 2), count)]


def assign_block(rng, own, number, rows, amount, top, most, lean):
    order = jax.random.permutation(rng, amount)
    heavy_load, usual = portions_of(amount, rows * top, most, lean, True), portions_of(amount, rows * top, most, lean, False)
    places = jnp.arange(amount)

    def named(lengths, offset_by):
        used = int((lengths > 0).sum())
        fixed = max(1, used // 4)
        shifted = fixed + (places - fixed + offset_by * (used - fixed)) % max(1, amount - fixed)
        return jnp.zeros((amount,), jnp.int32).at[order[jnp.where(places < fixed, places, shifted)]].set(jnp.asarray(lengths, jnp.int32))

    lengths = jnp.where(number % 4 == 0, named(heavy_load, number // 4), named(usual, number - number // 4 - 1))
    mixed = jax.random.permutation(jax.random.fold_in(own, 3), amount)
    donor, receiver = mixed[0:amount // 2 * 2:2], mixed[1:amount // 2 * 2:2]
    room = jnp.minimum(lengths[donor] - 1, most - lengths[receiver]) // 2
    room = jnp.where((donor == order[0]) | (receiver == order[0]) | (lengths[receiver] == 0), 0, jnp.maximum(room, 0))
    shifted = jax.random.randint(jax.random.fold_in(own, 4), (amount // 2,), 0, 1 << 20) % (room + 1)
    lengths = lengths.at[donor].add(-shifted).at[receiver].add(shifted)
    items = jnp.searchsorted(jnp.cumsum(lengths), jnp.arange(rows * top), side="right").astype(jnp.int32)
    table = items.reshape(top, rows).T
    table = table[jax.random.permutation(jax.random.fold_in(own, 1), rows)]
    offset_by = jax.random.randint(jax.random.fold_in(own, 2), (rows, 1), 0, top)
    return jnp.take_along_axis(table, (jnp.arange(top)[None, :] + offset_by) % top, axis=1)


def portions_of(amount, total, limit, lean, full):
    loads = [(1 << 20) // math.isqrt(standing ** lean) + 1 for standing in range(1, amount + 1)]
    largest = limit if full else min(limit, max(-(-total // amount), total * loads[0] // sum(loads)))
    least = 1 if total - largest >= amount - 1 else 0
    given, surplus = [largest] + [least] * (amount - 1), total - largest - least * (amount - 1)
    while surplus > 0:
        movable = [i for i in range(1, amount) if given[i] < largest] or [i for i in range(1, amount) if given[i] < limit]
        whole, remaining = sum([loads[i] for i in movable]), surplus
        for i in movable:
            addition = min(limit - given[i], max(1, remaining * loads[i] // whole), surplus)
            given[i] = given[i] + addition
            surplus = surplus - addition
    return np.array(given)


def normal_values(key, extent, spread, reach, cuts=(), kind=jnp.bfloat16):
    array = jax.random.normal(key, extent, jnp.float32) * spread
    if len(cuts) > 0:
        array = steps_of(key, extent, cuts, -0.22, 0.18) * array
    return jnp.clip(array, min=-reach, max=reach).astype(kind)


def heavy_noise(own_key, shape, scale, reach, shards, heavy, kind=jnp.bfloat16):
    array = scale * jax.random.normal(own_key, shape, jnp.float32)
    if shards:
        array = array * steps_of(own_key, shape, shards, -0.22, 0.18)
    return jnp.clip(strengthened(array, jax.random.fold_in(own_key, 3), *heavy), -reach, reach).astype(kind)


def setup_inputs(seed: int = 0) -> dict:
    arg_keys = jax.random.split(jax.random.key(seed), 17)
    tokens = heavy_noise(arg_keys[0], (TOKENS, D), 1.0, 6.0, ((0, 8),), (0, 1, 8, 2.0))
    segments = jax.vmap(lambda own: jnp.searchsorted(jnp.cumsum(ragged(own, DOCS, LEN, LEN // 2, 2)), jnp.arange(LEN), side="right"))(jax.random.split(arg_keys[1], N_DP)).reshape((N_DP, LEN)).astype(jnp.int32)
    routes_keys = jax.random.split(jax.random.fold_in(arg_keys[2], 1), TOKENS // ROWS)
    routes_turns = jax.random.permutation(jax.random.fold_in(arg_keys[2], 3), TOKENS // ROWS)
    routes = jax.vmap(lambda own, number: assign_block(jax.random.fold_in(arg_keys[2], 2), own, number, ROWS, E, TOP, CAP, 1))(routes_keys, routes_turns).reshape((TOKENS, TOP))
    cotangent = normal_values(arg_keys[3], (TOKENS, D), 1.0, 6.0, ((0, 8),))
    norm_gain = jnp.clip(1.0 + 0.1 * jax.random.normal(arg_keys[4], (D,), jnp.float32), 0.5, 1.5)
    post_gain = jnp.clip(1.0 + 0.1 * jax.random.normal(arg_keys[5], (D,), jnp.float32), 0.5, 1.5)
    query_gain = jnp.clip(1.0 + 0.1 * jax.random.normal(arg_keys[6], (HD,), jnp.float32), 0.5, 1.5)
    key_gain = jnp.clip(1.0 + 0.1 * jax.random.normal(arg_keys[7], (HD,), jnp.float32), 0.5, 1.5)
    w_query = normal_values(arg_keys[8], (D, H * HD), D ** -0.5, 0.125, ((0, 4), (1, 4)))
    w_key = normal_values(arg_keys[9], (D, H * HD), D ** -0.5, 0.125, ((0, 4), (1, 4)))
    w_value = normal_values(arg_keys[10], (D, H * HD), D ** -0.5, 0.125, ((0, 4), (1, 4)))
    w_output = normal_values(arg_keys[11], (D, H * HD), (max(H * HD // 128, 2)) ** -0.5, 1.5, ((0, 4), (1, 4)))
    w_router = normal_values(arg_keys[12], (D, E), (4 * D) ** -0.5, 0.0625)
    w_gate = normal_values(arg_keys[13], (D, E, FFE), D ** -0.5, 0.125, ((0, 4), (2, 4)))
    w_up = normal_values(arg_keys[14], (D, E, FFE), D ** -0.5, 0.125, ((0, 4), (2, 4)))
    w_down = normal_values(arg_keys[15], (D, E, FFE), (max(FFE // 64, 2)) ** -0.5, 1.5, ((0, 4), (2, 4)))
    return {"tokens": tokens, "segments": segments, "routes": routes, "cotangent": cotangent, "norm_gain": norm_gain, "post_gain": post_gain, "query_gain": query_gain, "key_gain": key_gain, "w_query": w_query, "w_key": w_key, "w_value": w_value, "w_output": w_output, "w_router": w_router, "w_gate": w_gate, "w_up": w_up, "w_down": w_down}


NORM_EPSILON = 1e-05
MASKED = -1e+30
HIGHEST_MODE = lax.Precision.HIGHEST

@jax.custom_vjp
def low(v):
    return lax.optimization_barrier(v.astype(jnp.bfloat16)).astype(jnp.float32)

@jax.custom_vjp
def low_back(v):
    return v

def low_keep(v):
    return (low(v), None)

def low_pass(kept, grad):
    return (grad,)

def back_keep(v):
    return (v, None)

def back_low(kept, grad):
    return (low(grad),)
low.defvjp(low_keep, low_pass)
low_back.defvjp(back_keep, back_low)

def matmul(left, right):
    return jnp.dot(left, right, precision=HIGHEST_MODE, preferred_element_type=jnp.float32)

def rms_scale(values, gain_vec):
    return values * lax.rsqrt(lax.optimization_barrier(jnp.mean(values * values, axis=-1, keepdims=True)) + NORM_EPSILON) * gain_vec

def one_head(queries, keys, values, seg_row):
    scores = low_back(matmul(queries, keys.T) * HD ** (-0.5))
    scores = jnp.where(seg_row[:, None] == seg_row[None, :], scores, MASKED)
    weights = jax.nn.softmax(scores, axis=-1)
    return matmul(low(weights), values)

def one_sequence(pieces):
    queries, keys, values, seg_row = pieces

    def per_head(head_parts):
        return one_head(head_parts[0], head_parts[1], head_parts[2], seg_row)
    stacked = lax.map(jax.checkpoint(per_head), (jnp.swapaxes(queries, 0, 1), jnp.swapaxes(keys, 0, 1), jnp.swapaxes(values, 0, 1)))
    return jnp.swapaxes(stacked, 0, 1)

def forward(inputs, norm_gain, post_gain, query_gain, key_gain, w_query, w_key, w_value, w_output, w_router, w_gate, w_up, w_down, segments, routes):
    seq_count = segments.shape[0]
    seq_length = segments.shape[1]
    normed = low(rms_scale(inputs, norm_gain))

    def head_norm(projected, gain_vec):
        shaped = projected.reshape(seq_count, seq_length, H, HD)
        return low(rms_scale(shaped, gain_vec))
    queries = head_norm(low_back(matmul(normed, w_query)), query_gain)
    keys = head_norm(low_back(matmul(normed, w_key)), key_gain)
    values = low(low_back(matmul(normed, w_value))).reshape(seq_count, seq_length, H, HD)
    mixed = lax.map(jax.checkpoint(one_sequence), (queries, keys, values, segments))
    mixed = low(low_back(mixed.reshape(inputs.shape[0], H * HD)))
    attended = inputs + low_back(matmul(mixed, w_output.T))
    post = low(rms_scale(attended, post_gain))
    logits = low_back(matmul(post, w_router))
    route_probs = jax.nn.softmax(logits, axis=-1)
    picks = (routes[:, :, None] == jnp.arange(E, dtype=jnp.int32)[None, None, :]).astype(jnp.float32)
    gates = lax.optimization_barrier(jnp.sum(picks, axis=1)) * route_probs

    def expert_step(running, slices):
        gate_cols, up_cols, down_cols, weight_col = slices
        gated = low_back(matmul(post, gate_cols))
        lifted = low_back(matmul(post, up_cols))
        hidden = low(jax.nn.silu(gated) * lifted)
        result = low_back(matmul(hidden, down_cols.T))
        return (running + weight_col[:, None] * result, None)
    running, _ = lax.scan(jax.checkpoint(expert_step), jnp.zeros_like(inputs), (jnp.swapaxes(w_gate, 0, 1), jnp.swapaxes(w_up, 0, 1), jnp.swapaxes(w_down, 0, 1), gates.T))
    return attended + running

def reference(tokens, segments, routes, cotangent, norm_gain, post_gain, query_gain, key_gain, w_query, w_key, w_value, w_output, w_router, w_gate, w_up, w_down):
    floats = [item.astype(jnp.float32) for item in (tokens, norm_gain, post_gain, query_gain, key_gain, w_query, w_key, w_value, w_output, w_router, w_gate, w_up, w_down)]

    def forward_run(*arrays):
        return forward(*arrays, segments, routes)
    output, pullback = jax.vjp(forward_run, *floats)
    gradients = pullback(cotangent.astype(jnp.float32))
    return (output, gradients[0], gradients[1], gradients[2], gradients[3], gradients[4], gradients[5], gradients[6], gradients[7], gradients[8], gradients[9], gradients[10], gradients[11], gradients[12])
```

```python
import jax
import jax.numpy as jnp
from jax import lax
from jax.sharding import PartitionSpec as P

HD = 128


NORM_EPSILON = 1e-05
MASKED = -1e30


def rms_parts(values):
    inverse = lax.rsqrt(jnp.mean(values * values, axis=-1, keepdims=True) + NORM_EPSILON)
    return (values * inverse, inverse)


def rms_back(grad_normed, normed, inverse):
    return inverse * (grad_normed - normed * jnp.mean(grad_normed * normed, axis=-1, keepdims=True))


def contract_first(left, right):
    return lax.dot_general(
        left, right, (((0,), (0,)), ((), ())), preferred_element_type=jnp.float32
    )


def contract_last(left, right):
    return lax.dot_general(
        left, right, (((1,), (1,)), ((), ())), preferred_element_type=jnp.float32
    )


def silu_backs(hid_grad, gated, lifted):
    sigmoid_gate = jax.nn.sigmoid(gated)
    gate_grad = (hid_grad * lifted * sigmoid_gate * (1.0 + gated * (1.0 - sigmoid_gate))).astype(
        jnp.bfloat16
    )
    up_grad = (hid_grad * gated * sigmoid_gate).astype(jnp.bfloat16)
    return (gate_grad, up_grad)


def weights_gathered(
    tokens,
    segments,
    routes,
    cotangent,
    norm_gain,
    post_gain,
    query_gain,
    key_gain,
    w_query,
    w_key,
    w_value,
    w_output,
    w_router,
    w_gate,
    w_up,
    w_down,
):
    span_rows, model_width = tokens.shape
    slot_cap = 3 * span_rows // 4
    expert_count = w_router.shape[1]
    local_cols = w_query.shape[1]
    head_count = local_cols // HD
    score_scale = HD ** (-0.5)
    seg_row = segments[0]
    own_seg = lax.dynamic_slice_in_dim(seg_row, lax.axis_index("ctx") * span_rows, span_rows)
    input_f32 = tokens.astype(jnp.float32)
    cot_f32 = cotangent.astype(jnp.float32)
    normed1, inverse1 = rms_parts(input_f32)
    attn_in = (normed1 * norm_gain).astype(jnp.bfloat16)
    full_weights = (
        lax.all_gather(w_query, "dp", axis=0, tiled=True),
        lax.all_gather(w_key, "dp", axis=0, tiled=True),
        lax.all_gather(w_value, "dp", axis=0, tiled=True),
        lax.all_gather(w_output, "dp", axis=0, tiled=True),
        lax.all_gather(w_gate, "dp", axis=0, tiled=True),
        lax.all_gather(w_up, "dp", axis=0, tiled=True),
        lax.all_gather(w_down, "dp", axis=0, tiled=True),
    )
    full_query, full_key, full_value, full_output, full_gate, full_up, full_down = full_weights
    q_raw = jnp.dot(attn_in, full_query, preferred_element_type=jnp.float32).reshape(
        span_rows, head_count, HD
    )
    k_raw = jnp.dot(attn_in, full_key, preferred_element_type=jnp.float32).reshape(
        span_rows, head_count, HD
    )
    v_raw = jnp.dot(attn_in, full_value, preferred_element_type=jnp.float32)
    q_hat, q_inverse = rms_parts(q_raw)
    k_hat, k_inverse = rms_parts(k_raw)
    q_low = (q_hat * query_gain).astype(jnp.bfloat16)
    k_low = (k_hat * key_gain).astype(jnp.bfloat16).reshape(span_rows, local_cols)
    v_low = v_raw.astype(jnp.bfloat16)
    keys_all, values_all = (
        lax.all_gather(k_low, "ctx", axis=0, tiled=True),
        lax.all_gather(v_low, "ctx", axis=0, tiled=True),
    )
    seq_length = keys_all.shape[0]
    key_heads = keys_all.reshape(seq_length, head_count, HD)
    value_heads = values_all.reshape(seq_length, head_count, HD)
    same_doc = own_seg[:, None] == seg_row[None, :]
    scores = (
        jnp.einsum("qhd,khd->hqk", q_low, key_heads, preferred_element_type=jnp.float32)
        * score_scale
    )
    scores = jnp.where(same_doc[None], scores, MASKED)
    row_max = jnp.max(scores, axis=2, keepdims=True)
    exp_scores = jnp.exp(scores - row_max)
    row_total = jnp.sum(exp_scores, axis=2, keepdims=True)
    log_total = row_max + jnp.log(row_total)
    probs_low = (exp_scores / row_total).astype(jnp.bfloat16)
    mixed = jnp.einsum("hqk,khd->qhd", probs_low, value_heads, preferred_element_type=jnp.float32)
    mixed_low = mixed.reshape(span_rows, local_cols).astype(jnp.bfloat16)
    attn_part = contract_last(mixed_low, full_output)
    attended = input_f32 + lax.psum(attn_part.astype(jnp.bfloat16), "tensor").astype(jnp.float32)
    normed2, inverse2 = rms_parts(attended)
    post_low = (normed2 * post_gain).astype(jnp.bfloat16)
    logits = jnp.dot(post_low, w_router, preferred_element_type=jnp.float32)
    route_probs = jax.nn.softmax(logits, axis=-1)
    expert_ids = jnp.arange(expert_count, dtype=jnp.int32)
    chosen = jnp.any(routes[:, :, None] == expert_ids[None, None, :], axis=1)
    slot_index = jnp.cumsum(chosen.astype(jnp.int32), axis=0) - 1
    target = jnp.where(chosen, slot_index, slot_cap)
    token_grid = jnp.broadcast_to(
        jnp.arange(span_rows, dtype=jnp.int32)[:, None], (span_rows, expert_count)
    )
    expert_grid = jnp.broadcast_to(expert_ids[None, :], (span_rows, expert_count))
    slot_tokens = (
        jnp.zeros((expert_count, slot_cap + 1), jnp.int32)
        .at[expert_grid, target]
        .set(token_grid)[:, :slot_cap]
    )
    gate_values = jnp.where(chosen, route_probs, 0.0)
    slot_gate = (
        jnp.zeros((expert_count, slot_cap + 1), jnp.float32)
        .at[expert_grid, target]
        .set(gate_values)[:, :slot_cap]
    )
    routed_rows = post_low[slot_tokens]
    cot_rows = cotangent[slot_tokens]
    out_grad = (cot_rows * slot_gate[:, :, None]).astype(jnp.bfloat16)
    gated = jnp.einsum("ecd,def->ecf", routed_rows, full_gate, preferred_element_type=jnp.float32)
    lifted = jnp.einsum("ecd,def->ecf", routed_rows, full_up, preferred_element_type=jnp.float32)
    hidden = (jax.nn.silu(gated) * lifted).astype(jnp.bfloat16)
    result = jnp.einsum("ecf,def->ecd", hidden, full_down, preferred_element_type=jnp.float32)
    hid_grad = jnp.einsum("ecd,def->ecf", out_grad, full_down, preferred_element_type=jnp.float32)
    gate_grad, up_grad = silu_backs(hid_grad, gated, lifted)
    grad_gate_w = jnp.einsum(
        "ecd,ecf->def", routed_rows, gate_grad, preferred_element_type=jnp.float32
    )
    grad_up_w = jnp.einsum("ecd,ecf->def", routed_rows, up_grad, preferred_element_type=jnp.float32)
    grad_down_w = jnp.einsum("ecd,ecf->def", out_grad, hidden, preferred_element_type=jnp.float32)
    row_grad = jnp.einsum("ecf,def->ecd", gate_grad, full_gate, preferred_element_type=jnp.float32)
    row_grad = row_grad + jnp.einsum(
        "ecf,def->ecd", up_grad, full_up, preferred_element_type=jnp.float32
    )
    gate_part = jnp.sum(result * cot_rows, axis=2)
    moe_part = (
        jnp.zeros((span_rows, model_width), jnp.float32)
        .at[slot_tokens]
        .add(result * slot_gate[:, :, None])
    )
    moe_total, gate_grad_slots = (
        lax.psum(moe_part.astype(jnp.bfloat16), "tensor").astype(jnp.float32),
        lax.psum(gate_part.astype(jnp.bfloat16), "tensor").astype(jnp.float32),
    )
    output = attended + moe_total
    post_part = jnp.zeros((span_rows, model_width), jnp.float32).at[slot_tokens].add(row_grad)
    post_grad = lax.psum(post_part.astype(jnp.bfloat16), "tensor").astype(jnp.float32)
    padded_grad = jnp.concatenate(
        [gate_grad_slots, jnp.zeros((expert_count, 1), jnp.float32)], axis=1
    )
    prob_grad = jnp.where(chosen, padded_grad[expert_grid, target], 0.0)
    logit_grad = (
        route_probs * (prob_grad - jnp.sum(route_probs * prob_grad, axis=1, keepdims=True))
    ).astype(jnp.bfloat16)
    grad_router_w = contract_first(post_low, logit_grad)
    post_grad = post_grad + contract_last(logit_grad, w_router)
    grad_post = jnp.sum(post_grad * normed2, axis=0)
    attended_grad = cot_f32 + rms_back(post_grad * post_gain, normed2, inverse2)
    attn_grad = attended_grad.astype(jnp.bfloat16)
    grad_output_w = contract_first(attn_grad, mixed_low)
    mixed_grad = (
        jnp.dot(attn_grad, full_output, preferred_element_type=jnp.float32)
        .astype(jnp.bfloat16)
        .reshape(span_rows, head_count, HD)
    )
    row_delta = jnp.transpose(jnp.sum(mixed_grad * mixed, axis=2))[:, :, None]
    key_block = min(seq_length, 512)
    block_count = seq_length // key_block
    key_blocks = key_heads.reshape(block_count, key_block, head_count, HD)
    value_blocks = value_heads.reshape(block_count, key_block, head_count, HD)
    seg_blocks = seg_row.reshape(block_count, key_block)

    def key_step(query_grad, pieces):
        key_piece, value_piece, seg_piece = pieces
        raw_scores = (
            jnp.einsum("qhd,khd->hqk", q_low, key_piece, preferred_element_type=jnp.float32)
            * score_scale
        )
        key_mask = own_seg[:, None] == seg_piece[None, :]
        attn_probs = jnp.where(key_mask[None], jnp.exp(raw_scores - log_total), 0.0)
        prob_piece = jnp.einsum(
            "qhd,khd->hqk", mixed_grad, value_piece, preferred_element_type=jnp.float32
        )
        score_grad = (attn_probs * (prob_piece - row_delta)).astype(jnp.bfloat16)
        query_grad = (
            query_grad
            + jnp.einsum("hqk,khd->qhd", score_grad, key_piece, preferred_element_type=jnp.float32)
            * score_scale
        )
        key_piece_grad = (
            jnp.einsum("hqk,qhd->khd", score_grad, q_low, preferred_element_type=jnp.float32)
            * score_scale
        )
        value_piece_grad = jnp.einsum(
            "hqk,qhd->khd",
            attn_probs.astype(jnp.bfloat16),
            mixed_grad,
            preferred_element_type=jnp.float32,
        )
        return (
            query_grad,
            (
                key_piece_grad.reshape(key_block, local_cols),
                value_piece_grad.reshape(key_block, local_cols),
            ),
        )

    query_grad, (key_terms, value_terms) = lax.scan(
        key_step,
        jnp.zeros((span_rows, head_count, HD), jnp.float32),
        (key_blocks, value_blocks, seg_blocks),
    )
    key_grad_own, value_grad_own = (
        lax.psum_scatter(
            key_terms.reshape(seq_length, local_cols).astype(jnp.bfloat16),
            "ctx",
            scatter_dimension=0,
            tiled=True,
        ).astype(jnp.float32),
        lax.psum_scatter(
            value_terms.reshape(seq_length, local_cols).astype(jnp.bfloat16),
            "ctx",
            scatter_dimension=0,
            tiled=True,
        ).astype(jnp.float32),
    )

    def head_back(grad_low, hat_values, inverse, gain_vec):
        return (
            rms_back(grad_low * gain_vec, hat_values, inverse),
            jnp.sum(grad_low * hat_values, axis=(0, 1)),
        )

    q_grad, query_gain_grad = head_back(query_grad, q_hat, q_inverse, query_gain)
    k_grad, key_gain_grad = head_back(
        key_grad_own.reshape(span_rows, head_count, HD), k_hat, k_inverse, key_gain
    )
    q_grad_low = q_grad.reshape(span_rows, local_cols).astype(jnp.bfloat16)
    k_grad_low = k_grad.reshape(span_rows, local_cols).astype(jnp.bfloat16)
    v_grad_low = value_grad_own.astype(jnp.bfloat16)
    grad_query_w = contract_first(attn_in, q_grad_low)
    grad_key_w = contract_first(attn_in, k_grad_low)
    grad_value_w = contract_first(attn_in, v_grad_low)
    in_part = (
        contract_last(q_grad_low, full_query)
        + contract_last(k_grad_low, full_key)
        + contract_last(v_grad_low, full_value)
    )
    in_grad = lax.psum(in_part.astype(jnp.bfloat16), "tensor").astype(jnp.float32)
    grad_norm = jnp.sum(in_grad * normed1, axis=0)
    input_grad = attended_grad + rms_back(in_grad * norm_gain, normed1, inverse1)
    weight_grads = tuple(
        (
            lax.psum_scatter(
                grad_query_w.astype(jnp.bfloat16), ("dp", "ctx"), scatter_dimension=0, tiled=True
            ).astype(jnp.float32),
            lax.psum_scatter(
                grad_key_w.astype(jnp.bfloat16), ("dp", "ctx"), scatter_dimension=0, tiled=True
            ).astype(jnp.float32),
            lax.psum_scatter(
                grad_value_w.astype(jnp.bfloat16), ("dp", "ctx"), scatter_dimension=0, tiled=True
            ).astype(jnp.float32),
            lax.psum_scatter(
                grad_output_w.astype(jnp.bfloat16), ("dp", "ctx"), scatter_dimension=0, tiled=True
            ).astype(jnp.float32),
            lax.psum_scatter(
                grad_gate_w.astype(jnp.bfloat16), ("dp", "ctx"), scatter_dimension=0, tiled=True
            ).astype(jnp.float32),
            lax.psum_scatter(
                grad_up_w.astype(jnp.bfloat16), ("dp", "ctx"), scatter_dimension=0, tiled=True
            ).astype(jnp.float32),
            lax.psum_scatter(
                grad_down_w.astype(jnp.bfloat16), ("dp", "ctx"), scatter_dimension=0, tiled=True
            ).astype(jnp.float32),
        )
    )
    leader = (lax.axis_index("tensor") == 0).astype(jnp.float32)
    small_sums = lax.psum(
        (
            grad_router_w * leader,
            grad_norm * leader,
            grad_post * leader,
            query_gain_grad,
            key_gain_grad,
        ),
        ("dp", "ctx", "tensor"),
    )
    return (
        output,
        input_grad,
        small_sums[1],
        small_sums[2],
        small_sums[3],
        small_sums[4],
        weight_grads[0],
        weight_grads[1],
        weight_grads[2],
        weight_grads[3],
        small_sums[0],
        weight_grads[4],
        weight_grads[5],
        weight_grads[6],
    )


CORE_SWAP = ((0, 1), (1, 0), (2, 3), (3, 2))
CHIP_SWAP = ((0, 2), (2, 0), (1, 3), (3, 1))


def core_swap(values):
    return lax.ppermute(values, "tensor", CORE_SWAP)


def chip_swap(values):
    return lax.ppermute(values, "tensor", CHIP_SWAP)


def ctx_swap(values):
    return lax.ppermute(values, "ctx", ((0, 1), (1, 0)))


def dp_shift(values, amount, count):
    return lax.ppermute(values, "dp", tuple((i, (i + amount) % count) for i in range(count)))


def add_pair(left, right):
    return left.astype(jnp.float32) + right.astype(jnp.float32)


def sum_over_sequence(part):
    part = add_pair(part[:, :, 0], core_swap(part[:, :, 1])).astype(jnp.bfloat16)
    part = add_pair(part[:, 0], chip_swap(part[:, 1])).astype(jnp.bfloat16)
    return add_pair(part[0], ctx_swap(part[1]))


def spread_over_sequence(own):
    pair = jnp.stack([own, ctx_swap(own)])
    quad = jnp.stack([pair, chip_swap(pair)], axis=1)
    return jnp.stack([quad, core_swap(quad)], axis=2)


def spread_over_tensor(own, t_index):
    pair = jnp.stack([own, core_swap(own)])
    quad = jnp.concatenate([pair, chip_swap(pair)]).astype(jnp.float32)
    blocks = [lax.dynamic_index_in_dim(quad, t_index ^ r, keepdims=False) for r in range(4)]
    return jnp.concatenate(blocks)


def gather_tokens(own):
    part = lax.all_gather(own, ("dp", "ctx"), axis=0, tiled=True)
    return jnp.concatenate([part, core_swap(part)])


def scatter_tokens(part):
    half = part.shape[0] // 2
    mine = add_pair(part[:half], core_swap(part[half:])).astype(part.dtype)
    return lax.psum_scatter(mine, ("dp", "ctx"), scatter_dimension=0, tiled=True)


def experts_exchanged(
    tokens,
    segments,
    routes,
    cotangent,
    norm_gain,
    post_gain,
    query_gain,
    key_gain,
    w_query,
    w_key,
    w_value,
    w_output,
    w_router,
    w_gate,
    w_up,
    w_down,
):
    dp_count = lax.axis_size("dp")
    z_index, y_index, t_index = (lax.axis_index(name) for name in ("dp", "ctx", "tensor"))
    span_rows, model_width = tokens.shape
    own_rows = span_rows // 4
    expert_count = w_router.shape[1]
    held = expert_count // (dp_count * 2)
    local_depth, _, hidden_part = w_gate.shape
    head_cols = w_query.shape[1] // 2
    head_count = head_cols // HD
    score_scale = HD ** (-0.5)
    bf16, f32 = jnp.bfloat16, jnp.float32

    def relative(values):
        return jnp.concatenate(
            [
                lax.dynamic_slice_in_dim(values, (t_index ^ r) * own_rows, own_rows)
                for r in range(4)
            ]
        )

    tokens_own = relative(tokens)
    tokens_seq = jnp.concatenate([tokens_own, ctx_swap(tokens_own)])
    seg_row = segments[0]
    seg_rel = jnp.concatenate(
        [
            relative(lax.dynamic_slice_in_dim(seg_row, (y_index ^ a) * span_rows, span_rows))
            for a in range(2)
        ]
    )

    def head_slice(weight):
        return lax.dynamic_slice_in_dim(weight, y_index * head_cols, head_cols, axis=1)

    full_qkv = lax.all_gather(
        jnp.concatenate([head_slice(w_query), head_slice(w_key), head_slice(w_value)], axis=1),
        "dp",
        axis=0,
        tiled=True,
    )
    full_output = lax.all_gather(head_slice(w_output), "dp", axis=0, tiled=True)

    def own_experts(weight):
        by_place = weight.reshape(local_depth, dp_count, 2, held, hidden_part)
        mine = lax.dynamic_index_in_dim(by_place, y_index, axis=2, keepdims=False)
        mine = jnp.transpose(mine, (1, 0, 2, 3)).reshape(
            dp_count, local_depth, held * hidden_part
        )
        full = jnp.zeros((dp_count * local_depth, held * hidden_part), weight.dtype)
        for k in range(dp_count):
            piece = lax.dynamic_index_in_dim(
                mine, (z_index + k) % dp_count, axis=0, keepdims=False
            )
            if k:
                piece = dp_shift(piece, k, dp_count)
            source = (z_index - k) % dp_count
            full = lax.dynamic_update_slice_in_dim(full, piece, source * local_depth, axis=0)
        return full, chip_swap(full)

    gate_w = own_experts(w_gate)
    up_w = own_experts(w_up)
    down_w = own_experts(w_down)

    input_f32 = tokens_seq.astype(f32)
    normed1, inverse1 = rms_parts(input_f32)
    attn_in = (normed1 * norm_gain).astype(bf16)
    seq_length = attn_in.shape[0]
    qkv = jnp.dot(attn_in, full_qkv, preferred_element_type=f32)
    q_raw, k_raw, v_raw = (
        qkv[:, i * head_cols : (i + 1) * head_cols].reshape(seq_length, head_count, HD)
        for i in range(3)
    )
    q_hat, q_inverse = rms_parts(q_raw)
    k_hat, k_inverse = rms_parts(k_raw)
    q_low = (q_hat * query_gain).astype(bf16)
    k_low = (k_hat * key_gain).astype(bf16)
    v_low = v_raw.astype(bf16)
    same_doc = seg_rel[:, None] == seg_rel[None, :]

    def masked_scores():
        scores = jnp.einsum("qhd,khd->hqk", q_low, k_low, preferred_element_type=f32)
        return jnp.where(same_doc[None], scores * score_scale, MASKED)

    scores = masked_scores()
    row_max = jnp.max(scores, axis=2, keepdims=True)
    exp_scores = jnp.exp(scores - row_max)
    row_total = jnp.sum(exp_scores, axis=2, keepdims=True)
    probs = exp_scores / row_total
    probs_low = probs.astype(bf16)
    mixed = jnp.einsum("hqk,khd->qhd", probs_low, v_low, preferred_element_type=f32)
    mixed_low = mixed.reshape(seq_length, head_cols).astype(bf16)
    attn_part = contract_last(mixed_low, full_output).astype(bf16)
    attn_sum = sum_over_sequence(attn_part.reshape(2, 2, 2, own_rows, model_width))

    cot_own = lax.dynamic_slice_in_dim(cotangent, t_index * own_rows, own_rows)
    routes_own = lax.dynamic_slice_in_dim(routes, t_index * own_rows, own_rows)
    routes_next = lax.dynamic_slice_in_dim(routes, (t_index ^ 1) * own_rows, own_rows)
    attended = tokens_own[:own_rows].astype(f32) + attn_sum
    normed2, inverse2 = rms_parts(attended)
    post_low = (normed2 * post_gain).astype(bf16)
    expert_ids = jnp.arange(expert_count, dtype=jnp.int32)
    chosen = jnp.any(routes_own[:, :, None] == expert_ids[None, None, :], axis=1)
    route_probs = jax.nn.softmax(
        jnp.dot(post_low, w_router, preferred_element_type=f32), axis=-1
    )

    cot_all = gather_tokens(cot_own)
    routes_all = lax.all_gather(
        jnp.concatenate([routes_own, routes_next], axis=1), ("dp", "ctx"), axis=0, tiled=True
    )
    top = routes.shape[1]
    routes_all = jnp.concatenate([routes_all[:, :top], routes_all[:, top:]])
    post_all = gather_tokens(post_low)
    probs_all = jax.nn.softmax(
        jnp.dot(post_all, w_router, preferred_element_type=f32), axis=-1
    )
    first = (z_index * 2 + y_index) * held
    gate_cols = []
    for i in range(held):
        picked = jnp.any(routes_all == first + i, axis=1, keepdims=True)
        prob = jnp.sum(
            jnp.where(expert_ids[None, :] == first + i, probs_all, 0.0), axis=1, keepdims=True
        )
        gate_cols.append(jnp.where(picked, prob, 0.0))
    slot_of = jnp.arange(held * hidden_part, dtype=jnp.int32)[None, :] // hidden_part
    gate_wide = sum(jnp.where(slot_of == i, gate_cols[i], 0.0) for i in range(held))

    def expert_half(gate_half, up_half, down_half):
        gated = jnp.dot(post_all, gate_half, preferred_element_type=f32)
        lifted = jnp.dot(post_all, up_half, preferred_element_type=f32)
        back = jnp.dot(cot_all, down_half, preferred_element_type=f32)
        hidden = jax.nn.silu(gated) * lifted
        gate_grad, up_grad = silu_backs(back * gate_wide, gated, lifted)
        scored = hidden * back
        gate_sums = [
            jnp.sum(jnp.where(slot_of == i, scored, 0.0), axis=1, keepdims=True)
            for i in range(held)
        ]
        return (hidden * gate_wide).astype(bf16), gate_grad, up_grad, gate_sums

    halves = [expert_half(gate_w[i], up_w[i], down_w[i]) for i in range(2)]
    gate_part = sum(
        jnp.where(
            expert_ids[None, :] == first + i, halves[0][3][i] + halves[1][3][i], 0.0
        )
        for i in range(held)
    )
    gate_sum = scatter_tokens(gate_part)
    post_part = sum(
        contract_last(halves[i][1], gate_w[i]) + contract_last(halves[i][2], up_w[i])
        for i in range(2)
    )
    post_grad = scatter_tokens(post_part.astype(bf16)).astype(f32)
    moe_part = sum(contract_last(halves[i][0], down_w[i]) for i in range(2))
    moe_sum = scatter_tokens(moe_part.astype(bf16)).astype(f32)

    def own_grad(left, kind):
        own = contract_first(left, halves[0][kind])
        other = contract_first(left, halves[1][kind]).astype(bf16)
        total = add_pair(own, chip_swap(other)).astype(bf16)
        rows = local_depth // 2
        total = total.reshape(dp_count, 2, rows, held * hidden_part)
        keep = lax.dynamic_index_in_dim(total, y_index, axis=1, keepdims=False)
        give = lax.dynamic_index_in_dim(total, 1 - y_index, axis=1, keepdims=False)
        both = jnp.stack([keep, ctx_swap(give)], axis=1)
        full = jnp.zeros((dp_count, 2, held, rows, hidden_part), f32)
        for k in range(dp_count):
            piece = lax.dynamic_index_in_dim(
                both, (z_index + k) % dp_count, axis=0, keepdims=False
            )
            if k:
                piece = dp_shift(piece, k, dp_count)
            source = (z_index - k) % dp_count
            piece = jnp.transpose(
                piece.reshape(2, rows, held, hidden_part), (0, 2, 1, 3)
            ).astype(f32)
            for a in range(2):
                full = lax.dynamic_update_slice(
                    full,
                    piece[a][None, None],
                    (source, y_index ^ a, 0, 0, 0),
                )
        return jnp.transpose(
            full.reshape(expert_count, rows, hidden_part), (1, 0, 2)
        )

    grad_gate_w = own_grad(post_all, 1)
    grad_up_w = own_grad(post_all, 2)
    grad_down_w = own_grad(cot_all, 0)

    output = spread_over_tensor((attended + moe_sum).astype(bf16), t_index)
    prob_grad = jnp.where(chosen, gate_sum, 0.0)
    logit_grad = (
        route_probs * (prob_grad - jnp.sum(route_probs * prob_grad, axis=1, keepdims=True))
    ).astype(bf16)
    grad_router_w = contract_first(post_low, logit_grad)
    post_grad = post_grad + contract_last(logit_grad, w_router)
    grad_post = jnp.sum(post_grad * normed2, axis=0)
    attended_grad = cot_own.astype(f32) + rms_back(post_grad * post_gain, normed2, inverse2)

    attn_grad = spread_over_sequence(attended_grad.astype(bf16)).reshape(
        seq_length, model_width
    )
    grad_output_w = contract_first(attn_grad, mixed_low)
    mixed_grad = (
        jnp.dot(attn_grad, full_output, preferred_element_type=f32)
        .astype(bf16)
        .reshape(seq_length, head_count, HD)
    )
    row_delta = jnp.transpose(jnp.sum(mixed_grad * mixed, axis=2))[:, :, None]
    prob_back = jnp.einsum("qhd,khd->hqk", mixed_grad, v_low, preferred_element_type=f32)
    score_grad = (probs * (prob_back - row_delta)).astype(bf16)
    query_grad = score_scale * jnp.einsum(
        "hqk,khd->qhd", score_grad, k_low, preferred_element_type=f32
    )
    key_grad = score_scale * jnp.einsum(
        "hqk,qhd->khd", score_grad, q_low, preferred_element_type=f32
    )
    value_grad = jnp.einsum("hqk,qhd->khd", probs_low, mixed_grad, preferred_element_type=f32)

    def head_back(grad_low, hat_values, inverse, gain_vec):
        return (
            rms_back(grad_low * gain_vec, hat_values, inverse),
            jnp.sum(grad_low * hat_values, axis=(0, 1)),
        )

    q_grad, query_gain_grad = head_back(query_grad, q_hat, q_inverse, query_gain)
    k_grad, key_gain_grad = head_back(key_grad, k_hat, k_inverse, key_gain)
    qkv_grad = jnp.concatenate(
        [
            item.reshape(seq_length, head_cols).astype(bf16)
            for item in (q_grad, k_grad, value_grad)
        ],
        axis=1,
    )
    in_part = contract_last(qkv_grad, full_qkv).astype(bf16)
    in_grad = sum_over_sequence(in_part.reshape(2, 2, 2, own_rows, model_width))
    grad_qkv_w = contract_first(attn_in, qkv_grad)
    normed_own, inverse_own = normed1[:own_rows], inverse1[:own_rows]
    grad_norm = jnp.sum(in_grad * normed_own, axis=0)
    input_grad = attended_grad + rms_back(in_grad * norm_gain, normed_own, inverse_own)
    input_grad = spread_over_tensor(input_grad.astype(bf16), t_index)

    def attention_grad(part):
        mine = lax.psum_scatter(part.astype(bf16), "dp", scatter_dimension=0, tiled=True)
        rows = local_depth // 2
        mine = mine.reshape(2, rows, part.shape[1])
        keep = lax.dynamic_index_in_dim(mine, y_index, axis=0, keepdims=False)
        came = ctx_swap(lax.dynamic_index_in_dim(mine, 1 - y_index, axis=0, keepdims=False))
        low, high = jnp.where(y_index == 0, keep, came), jnp.where(y_index == 0, came, keep)
        return [
            jnp.concatenate([low[:, cols], high[:, cols]], axis=1).astype(f32)
            for cols in (
                slice(i * head_cols, (i + 1) * head_cols) for i in range(part.shape[1] // head_cols)
            )
        ]

    (grad_output_w,) = attention_grad(grad_output_w)
    grad_query_w, grad_key_w, grad_value_w = attention_grad(grad_qkv_w)
    small_sums = lax.psum(
        (grad_router_w, grad_norm, grad_post, query_gain_grad, key_gain_grad),
        ("dp", "ctx", "tensor"),
    )
    return (
        output,
        input_grad,
        small_sums[1],
        small_sums[2],
        small_sums[3],
        small_sums[4],
        grad_query_w,
        grad_key_w,
        grad_value_w,
        grad_output_w,
        small_sums[0],
        grad_gate_w,
        grad_up_w,
        grad_down_w,
    )


def on_device(*arrays):
    counts = tuple(lax.axis_size(name) for name in ("dp", "ctx", "tensor"))
    experts = arrays[12].shape[1]
    divides = counts[1:] == (2, 4) and experts % (counts[0] * 2) == 0
    return (experts_exchanged if divides else weights_gathered)(*arrays)


def solution(mesh):
    return jax.shard_map(
        on_device,
        mesh=mesh,
        in_specs=(
            P(("dp", "ctx"), None),
            P("dp", None),
            P(("dp", "ctx"), None),
            P(("dp", "ctx"), None),
            P(),
            P(),
            P(),
            P(),
            P("dp", "tensor"),
            P("dp", "tensor"),
            P("dp", "tensor"),
            P("dp", "tensor"),
            P(),
            P("dp", None, "tensor"),
            P("dp", None, "tensor"),
            P("dp", None, "tensor"),
        ),
        out_specs=(
            P(("dp", "ctx"), None),
            P(("dp", "ctx"), None),
            P(),
            P(),
            P(),
            P(),
            P(("dp", "ctx"), "tensor"),
            P(("dp", "ctx"), "tensor"),
            P(("dp", "ctx"), "tensor"),
            P(("dp", "ctx"), "tensor"),
            P(),
            P(("dp", "ctx"), None, "tensor"),
            P(("dp", "ctx"), None, "tensor"),
            P(("dp", "ctx"), None, "tensor"),
        ),
        check_vma=False,
    )
```
